32 devices in a mesh: groups: 2 (over y), wide: 4 (over z), narrow: 4 (over x, core).
Axes of the slice: x: 2, y: 2, z: 4, core: 2. Of those that a mesh axis runs over, the one named last changes fastest.
Arguments:
- hidden: bfloat16 [4096, 4096], P(('groups', 'wide')), parts along dimension 0, may hold values from -16 to 16
- w_qkv: bfloat16 [4096, 3, 2048], P('wide', None, 'narrow'), may hold values from -0.09375 to 0.09375
- w_out: bfloat16 [2048, 4096], P(None, 'wide'), may hold values from -0.125 to 0.125
- seg_ids: int32 [4096], P('groups'), parts along dimension 0, may hold values from 0 to 3, never falling along the last dimension, each value on 1 to 1024 neighbouring positions
- shift_heads: int32 [16], replicated, may hold values from 0 to 1, as said below
Outputs:
- layer_out: bfloat16 [4096, 4096], P(('groups', 'wide', 'narrow')), parts along dimension 0
The draws below stay inside these ranges and needn't reach their ends.
There are 2 independent parts, one for each index of `groups`. The reference program is written for one: setup_inputs(seed, part) draws one part's arguments, and reference() takes and returns one part's arrays. A program takes and returns all parts, laid end to end along the dimension named above; an argument that names none is the same for every part. Nothing has to cross between parts.
Inputs may be any that keep to these rules, and one draw needn't show every extreme that they name: `shift_heads`: exactly half of the heads are marked with 1, the others with 0. `seg_ids`: never falls along the window; every number occurs on 1 to 1024 consecutive tokens, one on exactly that many.
All inputs are finite; a program needn't handle non-finite values.
Results may differ from the reference program's by a relative error of at most 0.012.
Values may be sent and summed in bfloat16 or wider, within the bound.
A program may use at most 128 MiB of HBM per device.

```python
import math
import jax
import jax.numpy as jnp
import numpy as np
from jax import lax

D = 4096
HEAD_DIM = 128
HEADS = 16
GROUP = 512
SHIFT = 256
TOK_DEV = 512
TOKENS = 2048
N_WIDE = 4


def draw_hidden(key, part):
    first_key = jax.random.fold_in(jax.random.fold_in(key, 11), 0)
    result = jnp.clip(jax.random.normal(first_key, (TOKENS, D), jnp.float32), -6.0, 6.0)
    return result.astype(jnp.bfloat16)


def draw_shift_heads(key, part):
    order = jax.random.permutation(jax.random.fold_in(key, 23), HEADS)
    return (order < HEADS // 2).astype(jnp.int32)


def levels(own_key, extent, cuts, least, largest):
    def one(dim, parts):
        steps = jax.random.uniform(jax.random.fold_in(jax.random.fold_in(own_key, 6), dim), (parts,), jnp.float32, least / len(cuts), largest / len(cuts))
        return jnp.repeat(jnp.exp(steps), extent[dim] // parts).reshape((-1,) + (1,) * (len(extent) - dim - 1))

    loudness = one(*cuts[0])
    for cut in cuts[1:]:
        loudness = loudness * one(*cut)
    return loudness


def split_up(number_of, total, most, lean):
    loads = [(1 << 20) // math.isqrt(standing ** lean) + 1 for standing in range(2, number_of + 1)]
    surplus, holding = total - most - (number_of - 1), [1] * (number_of - 1)
    while surplus > 0:
        candidates = [i for i in range(number_of - 1) if holding[i] < most]
        mass, left = sum([loads[i] for i in candidates]), surplus
        for i in candidates:
            more = min(most - holding[i], max(1, left * loads[i] // mass), surplus)
            holding[i] = holding[i] + more
            surplus = surplus - more
    return np.array([most] + holding)


def uneven_parts(key, count, total, limit, slope):
    if count == 2:
        one = jax.random.randint(key, (), max(1, total - limit), min(limit, total - 1) + 1)
        return jnp.stack([one, total - one])
    sizes = jnp.asarray(split_up(count, total, limit, slope), jnp.int32)
    couples = (count - 1) // 2
    giver, taker = sizes[1:1 + 2 * couples:2], sizes[2:2 + 2 * couples:2]
    slack = jnp.minimum(giver - 1, limit - taker)
    passed = jax.random.randint(jax.random.fold_in(key, 1), (couples,), 0, 1 << 20) % (slack + 1)
    sizes = sizes.at[1:1 + 2 * couples:2].set(giver - passed).at[2:2 + 2 * couples:2].set(taker + passed)
    return sizes[jax.random.permutation(jax.random.fold_in(key, 2), count)]


def centred(own_key, extent, spread, bound, cuts=(), kind=jnp.bfloat16):
    factor_of = levels(own_key, extent, cuts, -0.22, 0.18) if cuts else 1.0
    values = jax.random.normal(own_key, extent, jnp.float32) * spread * factor_of
    return jnp.minimum(jnp.maximum(values, -bound), bound).astype(kind)


def setup_inputs(seed: int = 0, part: int = 0) -> dict:
    keys = jax.random.split(jax.random.key(seed), 6)
    own_keys = jax.random.split(jax.random.fold_in(keys[5], part), 6)
    hidden = draw_hidden(jax.random.fold_in(jax.random.fold_in(keys[5], part), 71), part)
    w_qkv = centred(keys[1], (D, 3, HEADS * HEAD_DIM), D ** -0.5, 0.09375, ((0, 4), (2, 4)))
    w_out = centred(keys[2], (HEADS * HEAD_DIM, D), (HEADS * HEAD_DIM) ** -0.5, 0.125, ((1, 4),))
    seg_ids = jnp.searchsorted(jnp.cumsum(uneven_parts(own_keys[3], N_WIDE, TOKENS, 2 * TOK_DEV, 2)), jnp.arange(TOKENS), side="right").astype(jnp.int32)
    shift_heads = draw_shift_heads(jax.random.fold_in(keys[5], 71), part)
    return dict(hidden=hidden, w_qkv=w_qkv, w_out=w_out, seg_ids=seg_ids, shift_heads=shift_heads)


masked_out = -1e+30

def attend(query_rows, key_rows, value_rows, allowed):
    scores = jnp.einsum('ihd,jhd->hij', query_rows.astype(jnp.float32), key_rows.astype(jnp.float32)) * (1.0 / math.sqrt(HEAD_DIM))
    scores = jnp.where(allowed, scores, masked_out)
    row_max = lax.optimization_barrier(jnp.max(scores, axis=-1, keepdims=True))
    exponent = jnp.exp(scores - row_max)
    weights = (exponent / lax.optimization_barrier(jnp.sum(exponent, axis=-1, keepdims=True))).astype(jnp.bfloat16)
    combined = jnp.einsum('hij,jhd->ihd', weights.astype(jnp.float32), value_rows.astype(jnp.float32))
    return combined.astype(jnp.bfloat16)

def reference(hidden, w_qkv, w_out, seg_ids, shift_heads):
    width = HEADS * HEAD_DIM
    projected = jnp.dot(hidden, w_qkv.reshape(D, 3 * width), preferred_element_type=jnp.float32).astype(jnp.bfloat16)
    projected = projected.reshape(TOKENS, 3, HEADS, HEAD_DIM)
    shifted = shift_heads > 0
    moved_qkv = jnp.where(shifted[None, None, :, None], jnp.roll(projected, -SHIFT, axis=0), projected)
    seg_heads = jnp.where(shifted[:, None], jnp.roll(seg_ids, -SHIFT)[None, :], seg_ids[None, :])
    groups_all = TOKENS // GROUP
    blocks = moved_qkv.reshape(groups_all, GROUP, 3, HEADS, HEAD_DIM)
    block_segs = seg_heads.reshape(HEADS, groups_all, GROUP).transpose(1, 0, 2)
    positions = jnp.arange(GROUP, dtype=jnp.int32)
    causal = positions[:, None] >= positions[None, :]

    def one_group(inputs):
        block_qkv, block_seg = inputs
        allowed = causal[None] & (block_seg[:, :, None] == block_seg[:, None, :])
        return attend(block_qkv[:, 0], block_qkv[:, 1], block_qkv[:, 2], allowed)
    rolled_out = lax.map(one_group, (blocks, block_segs)).reshape(TOKENS, HEADS, HEAD_DIM)
    attended = jnp.where(shifted[None, :, None], jnp.roll(rolled_out, SHIFT, axis=0), rolled_out)
    return jnp.dot(attended.reshape(TOKENS, width), w_out, preferred_element_type=jnp.float32).astype(jnp.bfloat16)
```

```python
import functools
import math

import jax
import jax.numpy as jnp
from jax import lax
from jax.experimental import pallas as pl
from jax.experimental.pallas import tpu as pltpu
from jax.sharding import PartitionSpec as P

HEAD_DIM = 128
GROUP = 512
SHIFT = 256

masked_out = -1e30
MESH = pl.DeviceIdType.MESH


def gather_kernel(
    n, chunks, hidden_ref, wq_ref, wo_ref, proj_ref, wo_out,
    wbuf, acc, local_sem,
    send_r, send_l, send_yr, send_yl, recv_r, recv_l, recv_yr, recv_yl,
):
    me = lax.axis_index("wide")
    y = lax.axis_index("groups")
    other = 1 - y
    depth = wq_ref.shape[1]
    rows = depth // chunks
    steps = (n - 1) * chunks

    barrier = pltpu.get_barrier_semaphore()

    @pl.when(me > 0)
    def _():
        pl.semaphore_signal(barrier, inc=1, device_id={"wide": me - 1}, device_id_type=MESH)

    @pl.when(me < n - 1)
    def _():
        pl.semaphore_signal(barrier, inc=1, device_id={"wide": me + 1}, device_id_type=MESH)

    pl.semaphore_signal(barrier, inc=1, device_id={"groups": other}, device_id_type=MESH)
    has_left = jnp.where(me > 0, 1, 0)
    has_right = jnp.where(me < n - 1, 1, 0)
    own = [
        pltpu.make_async_copy(
            wq_ref.at[h], wbuf.at[h, pl.ds(pl.multiple_of(me * depth, depth), depth)], local_sem.at[h]
        )
        for h in range(2)
    ]
    own.append(pltpu.make_async_copy(wo_ref, wo_out.at[me], local_sem.at[2]))
    for copy in own:
        copy.start()
    pl.semaphore_wait(barrier, has_left + has_right + 1)

    def w_at(shard, half, c):
        start = pl.multiple_of(shard * depth + c * rows, rows)
        return wbuf.at[half, pl.ds(start, rows)]

    def wq_own(c):
        return wq_ref.at[y, pl.ds(pl.multiple_of(c * rows, rows), rows)]

    def o_at(shard, half):
        return wo_out.at[shard, half]

    def remote(src, dst, send, recv, slot, device):
        return pltpu.make_async_remote_copy(
            src_ref=src, dst_ref=dst, send_sem=send.at[slot], recv_sem=recv.at[slot],
            device_id=device, device_id_type=MESH,
        )

    right, left, across = {"wide": me + 1}, {"wide": me - 1}, {"groups": other}

    def pick(t):
        return t // chunks, lax.rem(t, chunks)

    def send_right(t, src, shard):
        s, c = pick(t)
        return remote(src, w_at(shard, y, c), send_r, recv_r, t, right)

    def send_left(t, src, shard):
        s, c = pick(t)
        return remote(src, w_at(shard, y, c), send_l, recv_l, t, left)

    @pl.loop(0, chunks)
    def _(c):
        @pl.when(me < n - 1)
        def _():
            send_right(c, wq_own(c), me).start()

        @pl.when(me > 0)
        def _():
            send_left(c, wq_own(c), me).start()

    acc[...] = jnp.zeros_like(acc)
    own[0].wait()
    own[1].wait()

    def add(shard, half, c):
        start = pl.multiple_of(shard * depth + c * rows, rows)
        acc[half] += jnp.dot(
            hidden_ref[:, pl.ds(start, rows)], wbuf[half, pl.ds(start, rows)],
            preferred_element_type=jnp.float32,
        )

    @pl.loop(0, 2 * chunks)
    def _(i):
        add(me, i // chunks, lax.rem(i, chunks))

    def from_across(t):
        s, c = pick(t)

        @pl.when(me - 1 - s >= 0)
        def _():
            ref = w_at(me - 1 - s, other, c)
            remote(ref, ref, send_yr, recv_yr, t, across).wait_recv()
            add(me - 1 - s, other, c)

        @pl.when(me + 1 + s <= n - 1)
        def _():
            ref = w_at(me + 1 + s, other, c)
            remote(ref, ref, send_yl, recv_yl, t, across).wait_recv()
            add(me + 1 + s, other, c)

    @pl.loop(0, steps)
    def _(t):
        s, c = pick(t)

        @pl.when(me - 1 - s >= 0)
        def _():
            ref = w_at(me - 1 - s, y, c)
            remote(ref, ref, send_r, recv_r, t, left).wait_recv()

            @pl.when(me < n - 1)
            def _():
                send_right(t + chunks, ref, me - 1 - s).start()

            remote(ref, ref, send_yr, recv_yr, t, across).start()

        @pl.when(me + 1 + s <= n - 1)
        def _():
            ref = w_at(me + 1 + s, y, c)
            remote(ref, ref, send_l, recv_l, t, right).wait_recv()

            @pl.when(me > 0)
            def _():
                send_left(t + chunks, ref, me + 1 + s).start()

            remote(ref, ref, send_yl, recv_yl, t, across).start()

        @pl.when(me - 1 - s >= 0)
        def _():
            add(me - 1 - s, y, c)

        @pl.when(me + 1 + s <= n - 1)
        def _():
            add(me + 1 + s, y, c)

        @pl.when(t > 0)
        def _():
            from_across(t - 1)

    @pl.when(me < n - 1)
    def _():
        remote(wo_ref.at[y], o_at(me, y), send_r, recv_r, steps, right).start()

    @pl.when(me > 0)
    def _():
        remote(wo_ref.at[y], o_at(me, y), send_l, recv_l, steps, left).start()

    from_across(steps - 1)
    proj_ref[...] = acc[...].astype(jnp.bfloat16)

    @pl.loop(0, n - 1)
    def _(s):
        t = steps + s

        @pl.when(me - 1 - s >= 0)
        def _():
            ref = o_at(me - 1 - s, y)
            remote(ref, ref, send_r, recv_r, t, left).wait_recv()

            @pl.when(me < n - 1)
            def _():
                remote(ref, ref, send_r, recv_r, t + 1, right).start()

            remote(ref, ref, send_yr, recv_yr, t, across).start()

        @pl.when(me + 1 + s <= n - 1)
        def _():
            ref = o_at(me + 1 + s, y)
            remote(ref, ref, send_l, recv_l, t, right).wait_recv()

            @pl.when(me > 0)
            def _():
                remote(ref, ref, send_l, recv_l, t + 1, left).start()

            remote(ref, ref, send_yl, recv_yl, t, across).start()

    own[2].wait()

    @pl.loop(0, n - 1)
    def _(s):
        t = steps + s

        @pl.when(me - 1 - s >= 0)
        def _():
            ref = o_at(me - 1 - s, other)
            remote(ref, ref, send_yr, recv_yr, t, across).wait_recv()
            ref = o_at(me - 1 - s, y)
            remote(ref, ref, send_yr, recv_yr, t, across).wait_send()

        @pl.when(me + 1 + s <= n - 1)
        def _():
            ref = o_at(me + 1 + s, other)
            remote(ref, ref, send_yl, recv_yl, t, across).wait_recv()
            ref = o_at(me + 1 + s, y)
            remote(ref, ref, send_yl, recv_yl, t, across).wait_send()

        @pl.when(jnp.logical_and(me - s >= 0, me < n - 1))
        def _():
            ref = o_at(me - s, y)
            remote(ref, ref, send_r, recv_r, t, right).wait_send()

        @pl.when(jnp.logical_and(me + s <= n - 1, me > 0))
        def _():
            ref = o_at(me + s, y)
            remote(ref, ref, send_l, recv_l, t, left).wait_send()

    @pl.loop(0, steps)
    def _(t):
        s, c = pick(t)

        @pl.when(me - 1 - s >= 0)
        def _():
            ref = w_at(me - 1 - s, y, c)
            remote(ref, ref, send_yr, recv_yr, t, across).wait_send()

        @pl.when(me + 1 + s <= n - 1)
        def _():
            ref = w_at(me + 1 + s, y, c)
            remote(ref, ref, send_yl, recv_yl, t, across).wait_send()

        @pl.when(jnp.logical_and(me - s >= 0, me < n - 1))
        def _():
            ref = w_at(me - s, y, c)
            remote(ref, ref, send_r, recv_r, t, right).wait_send()

        @pl.when(jnp.logical_and(me + s <= n - 1, me > 0))
        def _():
            ref = w_at(me + s, y, c)
            remote(ref, ref, send_l, recv_l, t, left).wait_send()


def gather_project(hidden, wq, wo):
    n = lax.axis_size("wide")
    tok, width = hidden.shape
    half = wq.shape[2]
    chunks = max(1, wq.shape[1] // 256)
    slots = (n - 1) * (chunks + 1)
    vmem = pl.BlockSpec(memory_space=pltpu.VMEM)
    hbm = pl.BlockSpec(memory_space=pl.ANY)
    return pl.pallas_call(
        functools.partial(gather_kernel, n, chunks),
        out_shape=(
            jax.ShapeDtypeStruct((2, tok, half), jnp.bfloat16),
            jax.ShapeDtypeStruct((n,) + wo.shape, jnp.bfloat16),
        ),
        in_specs=[vmem, hbm, hbm],
        out_specs=(vmem, vmem),
        scratch_shapes=[
            pltpu.VMEM((2, width, half), jnp.bfloat16),
            pltpu.VMEM((2, tok, half), jnp.float32),
            pltpu.SemaphoreType.DMA((3,)),
        ]
        + [pltpu.SemaphoreType.DMA((slots,)) for _ in range(8)],
        compiler_params=pltpu.CompilerParams(
            collective_id=0, has_side_effects=True, vmem_limit_bytes=56 * 1024 * 1024
        ),
    )(hidden, wq, wo)


def attend_kernel(heads, blocks, q_ref, k_ref, v_ref, segq_ref, segk_ref, out_ref):
    rows = lax.broadcasted_iota(jnp.int32, (SHIFT, 2 * SHIFT), 0)
    cols = lax.broadcasted_iota(jnp.int32, (SHIFT, 2 * SHIFT), 1)
    causal = cols <= rows + SHIFT
    for h in range(heads):
        lanes = slice(h * HEAD_DIM, (h + 1) * HEAD_DIM)
        for b in range(blocks):
            mine = slice(b * SHIFT, (b + 1) * SHIFT)
            seen = slice(b * SHIFT, (b + 2) * SHIFT)
            scores = lax.dot_general(
                q_ref[mine, lanes], k_ref[seen, lanes], (((1,), (1,)), ((), ())),
                preferred_element_type=jnp.float32,
            ) * (1.0 / math.sqrt(HEAD_DIM))
            allowed = causal & (segq_ref[mine, :] == segk_ref[h, b])
            scores = jnp.where(allowed, scores, masked_out)
            exponent = jnp.exp(scores - jnp.max(scores, axis=-1, keepdims=True))
            weights = exponent / jnp.sum(exponent, axis=-1, keepdims=True)
            out_ref[mine, lanes] = jnp.dot(
                weights.astype(jnp.bfloat16), v_ref[seen, lanes], preferred_element_type=jnp.float32
            ).astype(jnp.bfloat16)


def per_device(hidden, w_qkv, w_out, seg_ids, shift_heads):
    n = lax.axis_size("wide")
    tok_rows = hidden.shape[0]
    depth, _, local_f = w_qkv.shape
    heads_here = local_f // HEAD_DIM
    blocks = tok_rows // SHIFT
    narrow_idx = lax.axis_index("narrow")
    first_tok = lax.axis_index("wide") * tok_rows
    shifted = lax.dynamic_slice_in_dim(shift_heads, narrow_idx * heads_here, heads_here) > 0

    half = 3 * local_f // 2
    wq = w_qkv.reshape(depth, 2, half).transpose(1, 0, 2)
    own_rows = lax.dynamic_slice_in_dim(w_out, narrow_idx * local_f, local_f, 0)
    wo = own_rows.reshape(2, local_f // 2, -1)
    proj, wo_all = gather_project(hidden, wq, wo)
    projected = jnp.concatenate([proj[0], proj[1]], 1)
    q = projected[:, :local_f]
    kv = projected[:, local_f:]
    before = lax.ppermute(kv[tok_rows - SHIFT :], "wide", [(i, (i + 1) % n) for i in range(n)])
    kv = jnp.concatenate([before, kv], 0)

    doubled = jnp.concatenate([seg_ids[-SHIFT:], seg_ids], 0)
    seg_here = lax.dynamic_slice_in_dim(doubled, first_tok, tok_rows + SHIFT)
    seg_q = seg_here[SHIFT:, None]
    windows = jnp.stack([seg_here[b * SHIFT : (b + 2) * SHIFT] for b in range(blocks)])
    odd = (jnp.arange(blocks) % 2 == 1)[None, :, None]
    reaches = (shifted[:, None, None] != odd) | (jnp.arange(2 * SHIFT) >= SHIFT)[None, None, :]
    seg_k = jnp.where(reaches, windows[None], -1)[:, :, None, :]

    vmem = pl.BlockSpec(memory_space=pltpu.VMEM)
    attended = pl.pallas_call(
        functools.partial(attend_kernel, heads_here, blocks),
        out_shape=jax.ShapeDtypeStruct((tok_rows, local_f), jnp.bfloat16),
        in_specs=[vmem] * 5,
        out_specs=vmem,
    )(q, kv[:, :local_f], kv[:, local_f:], seg_q, seg_k)

    partial_value = jnp.einsum(
        "tf,nfc->tnc", attended, wo_all.reshape(n, local_f, -1), preferred_element_type=jnp.float32
    ).astype(jnp.bfloat16).reshape(tok_rows, -1)
    return lax.psum_scatter(partial_value, "narrow", scatter_dimension=0, tiled=True)


def solution(mesh):
    placed = (
        P(("groups", "wide"), None),
        P("wide", None, "narrow"),
        P(None, "wide"),
        P("groups"),
        P(),
    )
    return jax.shard_map(
        per_device,
        mesh=mesh,
        in_specs=placed,
        out_specs=P(("groups", "wide", "narrow"), None),
        check_vma=False,
    )
```

```python
import functools
import math

import jax
import jax.numpy as jnp
from jax import lax
from jax.experimental import pallas as pl
from jax.experimental.pallas import tpu as pltpu
from jax.sharding import PartitionSpec as P

HEAD_DIM = 128
GROUP = 512
SHIFT = 256

masked_out = -1e30
MESH = pl.DeviceIdType.MESH
ROWS = 128
WO_CHUNKS = 2


def layer_kernel(
    n, narrow, chunks, wo_chunks,
    hidden_ref, wq_ref, wo_ref, segq_ref, segk_ref, out_ref,
    wbuf, acc, wo_buf, q_buf, kv_buf, att, part, pair_in, pair_sum, far_in,
    own_sem,
    qs_r, qs_l, qr, qs_y, qr_y,
    os_r, os_l, o_r, os_y, or_y,
    kv_sem, pair_s, pair_r, far_s, far_r,
):
    me = lax.axis_index("wide")
    y = lax.axis_index("groups")
    spot = lax.axis_index("narrow")
    other = 1 - y
    across_n = narrow // 2
    high, low = spot // 2, lax.rem(spot, 2)
    depth = wq_ref.shape[1]
    half = wbuf.shape[3]
    tok = hidden_ref.shape[0]
    rows = depth // chunks
    steps = (n - 1) * chunks
    wo_rows = wo_buf.shape[2] // wo_chunks
    cols = wo_buf.shape[3]
    blocks = tok // SHIFT
    per_half = half // HEAD_DIM
    has_left, has_right = me > 0, me < n - 1
    right, left = {"wide": me + 1}, {"wide": me - 1}
    after, before = {"wide": lax.rem(me + 1, n)}, {"wide": lax.rem(me + n - 1, n)}
    opposite = {"groups": other}
    pair = {"narrow": high * 2 + 1 - low}
    far = [{"narrow": lax.rem(high + d, across_n) * 2 + low} for d in range(1, across_n)]
    far_from = [{"narrow": lax.rem(high + across_n - d, across_n) * 2 + low} for d in range(1, across_n)]

    barrier = pltpu.get_barrier_semaphore()
    greeted = [after, before, opposite, pair] + far
    for device in greeted:
        pl.semaphore_signal(barrier, inc=1, device_id=device, device_id_type=MESH)

    def w_at(shard, part_of, c):
        start = pl.multiple_of(shard * depth + c * rows, rows)
        return wbuf.at[part_of, :, pl.ds(start, rows)]

    def wq_own(c):
        return wq_ref.at[
            :, pl.ds(pl.multiple_of(c * rows, rows), rows), pl.ds(pl.multiple_of(y * half, half), half)
        ]

    def o_at(shard, part_of, c):
        return wo_buf.at[shard, part_of, pl.ds(pl.multiple_of(c * wo_rows, wo_rows), wo_rows)]

    def wo_own(c):
        return wo_ref.at[spot, y, pl.ds(pl.multiple_of(c * wo_rows, wo_rows), wo_rows)]

    def remote(src, dst, send, recv, device):
        return pltpu.make_async_remote_copy(
            src_ref=src, dst_ref=dst, send_sem=send, recv_sem=recv,
            device_id=device, device_id_type=MESH,
        )

    def q_right(shard, c, src=None):
        dst = w_at(shard, y, c)
        return remote(dst if src is None else src, dst, qs_r.at[shard, c], qr.at[shard, c], right)

    def q_left(shard, c, src=None):
        dst = w_at(shard, y, c)
        return remote(dst if src is None else src, dst, qs_l.at[shard, c], qr.at[shard, c], left)

    def q_across(shard, c, part_of):
        ref = w_at(shard, part_of, c)
        return remote(ref, ref, qs_y.at[shard, c], qr_y.at[shard, c], opposite)

    def o_right(shard, c, src=None):
        dst = o_at(shard, y, c)
        return remote(dst if src is None else src, dst, os_r.at[shard, c], o_r.at[shard, c], right)

    def o_left(shard, c, src=None):
        dst = o_at(shard, y, c)
        return remote(dst if src is None else src, dst, os_l.at[shard, c], o_r.at[shard, c], left)

    def o_across(shard, c, part_of):
        ref = o_at(shard, part_of, c)
        return remote(ref, ref, os_y.at[shard, c], or_y.at[shard, c], opposite)

    own = [
        pltpu.make_async_copy(
            wq_ref.at[:, :, pl.ds(h * half, half)],
            wbuf.at[h, :, pl.ds(pl.multiple_of(me * depth, depth), depth)],
            own_sem.at[h],
        )
        for h in range(2)
    ]
    own.append(pltpu.make_async_copy(wo_ref.at[spot], wo_buf.at[me], own_sem.at[2]))
    for copy in own:
        copy.start()
    pl.semaphore_wait(barrier, len(greeted))

    @pl.loop(0, chunks)
    def _(c):
        @pl.when(has_right)
        def _():
            q_right(me, c, wq_own(c)).start()

        @pl.when(has_left)
        def _():
            q_left(me, c, wq_own(c)).start()

    acc[...] = jnp.zeros_like(acc)
    own[0].wait()
    own[1].wait()

    def add(shard, part_of, c):
        start = pl.multiple_of(shard * depth + c * rows, rows)
        piece = hidden_ref[:, pl.ds(start, rows)]
        for i in range(3):
            acc[part_of, i] += jnp.dot(
                piece, wbuf[part_of, i, pl.ds(start, rows)], preferred_element_type=jnp.float32
            )

    @pl.loop(0, 2 * chunks)
    def _(i):
        add(me, i // chunks, lax.rem(i, chunks))

    def add_across(t):
        s, c = t // chunks, lax.rem(t, chunks)
        for there, shard in ((me - 1 - s >= 0, me - 1 - s), (me + 1 + s <= n - 1, me + 1 + s)):
            @pl.when(there)
            def _():
                q_across(shard, c, other).wait_recv()
                add(shard, other, c)

    @pl.loop(0, steps)
    def _(t):
        s, c = t // chunks, lax.rem(t, chunks)

        @pl.when(me - 1 - s >= 0)
        def _():
            q_right(me - 1 - s, c).wait_recv()

            @pl.when(has_right)
            def _():
                q_right(me - 1 - s, c).start()

            q_across(me - 1 - s, c, y).start()

        @pl.when(me + 1 + s <= n - 1)
        def _():
            q_left(me + 1 + s, c).wait_recv()

            @pl.when(has_left)
            def _():
                q_left(me + 1 + s, c).start()

            q_across(me + 1 + s, c, y).start()

        for there, shard in ((me - 1 - s >= 0, me - 1 - s), (me + 1 + s <= n - 1, me + 1 + s)):
            @pl.when(there)
            def _():
                add(shard, y, c)

        @pl.when(t > 0)
        def _():
            add_across(t - 1)

    add_across(steps - 1)
    for h in range(2):
        q_buf[h] = acc[h, 0].astype(jnp.bfloat16)
        for i in range(2):
            kv_buf[h, i, SHIFT:] = acc[h, 1 + i].astype(jnp.bfloat16)

    kv_copy = remote(
        kv_buf.at[:, :, pl.ds(tok, SHIFT)], kv_buf.at[:, :, pl.ds(0, SHIFT)],
        kv_sem.at[0], kv_sem.at[1], after,
    )
    kv_copy.start()

    @pl.loop(0, wo_chunks)
    def _(c):
        @pl.when(has_right)
        def _():
            o_right(me, c, wo_own(c)).start()

        @pl.when(has_left)
        def _():
            o_left(me, c, wo_own(c)).start()

    causal = lax.broadcasted_iota(jnp.int32, (SHIFT, 2 * SHIFT), 1) <= (
        lax.broadcasted_iota(jnp.int32, (SHIFT, 2 * SHIFT), 0) + SHIFT
    )

    def attend(h, b):
        lanes = slice((h % per_half) * HEAD_DIM, (h % per_half + 1) * HEAD_DIM)
        mine, seen = slice(b * SHIFT, (b + 1) * SHIFT), slice(b * SHIFT, (b + 2) * SHIFT)
        keys, values = kv_buf.at[h // per_half, 0], kv_buf.at[h // per_half, 1]
        scores = lax.dot_general(
            q_buf[h // per_half, mine, lanes], keys[seen, lanes], (((1,), (1,)), ((), ())),
            preferred_element_type=jnp.float32,
        ) * (1.0 / math.sqrt(HEAD_DIM))
        allowed = causal & (segq_ref[mine, :] == segk_ref[h, b])
        scores = jnp.where(allowed, scores, masked_out)
        exponent = jnp.exp(scores - jnp.max(scores, axis=-1, keepdims=True))
        weights = exponent / jnp.sum(exponent, axis=-1, keepdims=True)
        att[mine, h * HEAD_DIM : (h + 1) * HEAD_DIM] = jnp.dot(
            weights.astype(jnp.bfloat16), values[seen, lanes], preferred_element_type=jnp.float32
        ).astype(jnp.bfloat16)

    least = jnp.minimum(me, n - 1 - me)

    def block_of(k):
        turn = (k + 1) // 2
        near = jnp.where(lax.rem(k, 2) == 1, me - turn, me + turn)
        rest = jnp.where(me > least, me - (k - least), me + (k - least))
        return jnp.where(k <= 2 * least, near, rest)

    def pass_on(k):
        shard = block_of(k)

        @pl.loop(0, wo_chunks)
        def _(c):
            o_right(shard, c).wait_recv()

            @pl.when(jnp.logical_and(shard < me, has_right))
            def _():
                o_right(shard, c).start()

            @pl.when(jnp.logical_and(shard > me, has_left))
            def _():
                o_left(shard, c).start()

            o_across(shard, c, y).start()

    def pair_copy(shard, a):
        return remote(
            part.at[shard, a * 2 + 1 - low], pair_in.at[shard, a],
            pair_s.at[shard, a], pair_r.at[shard, a], pair,
        )

    def far_copy(shard, d):
        a = lax.rem(high + d, across_n)
        return remote(
            pair_sum.at[shard, a], far_in.at[shard, d - 1],
            far_s.at[shard, d - 1], far_r.at[shard, d - 1], far[d - 1],
        )

    def far_arrival(shard, d):
        return remote(
            pair_sum.at[shard, high], far_in.at[shard, d - 1],
            far_s.at[shard, d - 1], far_r.at[shard, d - 1], far_from[d - 1],
        )

    def multiply(k):
        shard = block_of(k)
        width = att.shape[1] // 2
        share = tok // narrow
        for p in range(narrow):
            a_rows = att[p * share : (p + 1) * share, :]
            total = jnp.dot(a_rows[:, :width], wo_buf[shard, 0], preferred_element_type=jnp.float32)
            total += jnp.dot(a_rows[:, width:], wo_buf[shard, 1], preferred_element_type=jnp.float32)
            part[shard, p] = total.astype(jnp.bfloat16)
        for a in range(across_n):
            pair_copy(shard, a).start()

    def sum_pair(k):
        shard = block_of(k)
        for a in range(across_n):
            pair_copy(shard, a).wait_recv()
            total = part[shard, a * 2 + low].astype(jnp.float32) + pair_in[shard, a].astype(jnp.float32)
            pair_sum[shard, a] = total.astype(jnp.bfloat16)
        for d in range(1, across_n):
            far_copy(shard, d).start()

    def finish(k):
        shard = block_of(k)
        total = part[shard, high * 2 + low].astype(jnp.float32) + pair_in[shard, high].astype(jnp.float32)
        for d in range(1, across_n):
            far_arrival(shard, d).wait_recv()
            total += far_in[shard, d - 1].astype(jnp.float32)
        out_ref[:, pl.ds(pl.multiple_of(shard * cols, cols), cols)] = total.astype(out_ref.dtype)

    heads = 2 * per_half
    for b in range(1, blocks):
        for h in range(heads):
            attend(h, b)
    pass_on(1)
    kv_copy.wait_recv()
    for h in range(heads):
        attend(h, 0)
    own[2].wait()
    multiply(0)

    @pl.loop(1, n)
    def _(k):
        @pl.when(k > 1)
        def _():
            pass_on(k)

        sum_pair(k - 1)

        @pl.when(k > 1)
        def _():
            finish(k - 2)

        shard = block_of(k)

        @pl.loop(0, wo_chunks)
        def _(c):
            o_across(shard, c, other).wait_recv()

        multiply(k)

    sum_pair(n - 1)
    finish(n - 2)
    finish(n - 1)

    kv_copy.wait_send()

    @pl.loop(0, n)
    def _(shard):
        for a in range(across_n):
            pair_copy(shard, a).wait_send()
        for d in range(1, across_n):
            far_copy(shard, d).wait_send()
        goes_right = jnp.logical_and(shard <= me, has_right)
        goes_left = jnp.logical_and(shard >= me, has_left)
        for count, to_right, to_left, to_other in (
            (chunks, q_right, q_left, q_across), (wo_chunks, o_right, o_left, o_across)
        ):
            @pl.loop(0, count)
            def _(c):
                @pl.when(goes_right)
                def _():
                    to_right(shard, c).wait_send()

                @pl.when(goes_left)
                def _():
                    to_left(shard, c).wait_send()

                @pl.when(shard != me)
                def _():
                    to_other(shard, c, y).wait_send()


def layer(hidden, wq, wo, seg_q, seg_k):
    n, narrow = lax.axis_size("wide"), lax.axis_size("narrow")
    tok, width = hidden.shape
    half = wq.shape[2] // 2
    chunks = max(1, wq.shape[1] // ROWS)
    wo_chunks = WO_CHUNKS
    cols = wo.shape[3]
    share = tok // narrow
    vmem = pl.BlockSpec(memory_space=pltpu.VMEM)
    hbm = pl.BlockSpec(memory_space=pl.ANY)
    dma = pltpu.SemaphoreType.DMA
    bf16 = jnp.bfloat16
    return pl.pallas_call(
        functools.partial(layer_kernel, n, narrow, chunks, wo_chunks),
        out_shape=jax.ShapeDtypeStruct((share, n * cols), bf16),
        in_specs=[vmem, hbm, hbm, vmem, vmem],
        out_specs=vmem,
        scratch_shapes=[
            pltpu.VMEM((2, 3, width, half), bf16),
            pltpu.VMEM((2, 3, tok, half), jnp.float32),
            pltpu.VMEM((n,) + wo.shape[1:], bf16),
            pltpu.VMEM((2, tok, half), bf16),
            pltpu.VMEM((2, 2, tok + SHIFT, half), bf16),
            pltpu.VMEM((tok, 2 * half), bf16),
            pltpu.VMEM((n, narrow, share, cols), bf16),
            pltpu.VMEM((n, narrow // 2, share, cols), bf16),
            pltpu.VMEM((n, narrow // 2, share, cols), bf16),
            pltpu.VMEM((n, max(1, narrow // 2 - 1), share, cols), bf16),
            dma((3,)),
        ]
        + [dma((n, chunks))] * 5
        + [dma((n, wo_chunks))] * 5
        + [dma((2,))]
        + [dma((n, narrow // 2))] * 2
        + [dma((n, max(1, narrow // 2 - 1)))] * 2,
        compiler_params=pltpu.CompilerParams(
            collective_id=0, has_side_effects=True, vmem_limit_bytes=58 * 1024 * 1024
        ),
    )(hidden, wq, wo, seg_q, seg_k)


def per_device(hidden, w_qkv, w_out, seg_ids, shift_heads):
    tok_rows = hidden.shape[0]
    local_f = w_qkv.shape[2]
    heads_here = local_f // HEAD_DIM
    blocks = tok_rows // SHIFT
    narrow = lax.axis_size("narrow")
    first_tok = lax.axis_index("wide") * tok_rows
    shifted = lax.dynamic_slice_in_dim(shift_heads, lax.axis_index("narrow") * heads_here, heads_here) > 0

    doubled = jnp.concatenate([seg_ids[-SHIFT:], seg_ids], 0)
    seg_here = lax.dynamic_slice_in_dim(doubled, first_tok, tok_rows + SHIFT)
    seg_q = seg_here[SHIFT:, None]
    windows = jnp.stack([seg_here[b * SHIFT : (b + 2) * SHIFT] for b in range(blocks)])
    odd = (jnp.arange(blocks) % 2 == 1)[None, :, None]
    reaches = (shifted[:, None, None] != odd) | (jnp.arange(2 * SHIFT) >= SHIFT)[None, None, :]
    seg_k = jnp.where(reaches, windows[None], -1)[:, :, None, :]

    wq = w_qkv.transpose(1, 0, 2)
    wo = w_out.reshape(narrow, 2, local_f // 2, -1)
    return layer(hidden, wq, wo, seg_q, seg_k)


def solution(mesh):
    placed = (
        P(("groups", "wide"), None),
        P("wide", None, "narrow"),
        P(None, "wide"),
        P("groups"),
        P(),
    )
    return jax.shard_map(
        per_device,
        mesh=mesh,
        in_specs=placed,
        out_specs=P(("groups", "wide", "narrow"), None),
        check_vma=False,
    )
```

```python
import functools
import math

import jax
import jax.numpy as jnp
from jax import lax
from jax.experimental import pallas as pl
from jax.experimental.pallas import tpu as pltpu
from jax.sharding import PartitionSpec as P

HEAD_DIM = 128
GROUP = 512
SHIFT = 256

masked_out = -1e30
MESH = pl.DeviceIdType.MESH
ROWS = 256
WO_CHUNKS = 4
NEXT_EARLY = 1


def layer_kernel(
    n, narrow, chunks, wo_chunks,
    hidden_ref, wq_ref, wo_ref, segq_ref, segk_ref, out_ref,
    wbuf, acc, wo_buf, q_buf, kv_buf, att, part, pair_in, pair_sum, far_in,
    lent, help_out, help_in,
    own_sem, own_wo,
    qs_r, qs_l, qr, qs_y, qr_y,
    os_r, os_l, o_r, os_y, or_y,
    kv_sem, pair_s, pair_r, far_s, far_r,
    lend_sem, share_s, share_r, help_s, help_r,
):
    me = lax.axis_index("wide")
    y = lax.axis_index("groups")
    spot = lax.axis_index("narrow")
    other = 1 - y
    across_n = narrow // 2
    high, low = spot // 2, lax.rem(spot, 2)
    depth = wq_ref.shape[1]
    heads = wbuf.shape[0]
    phases = heads // 2
    tok = hidden_ref.shape[0]
    share = tok // narrow
    rows = depth // chunks
    steps = (n - 2) * chunks
    wo_rows = wo_buf.shape[2] // wo_chunks
    cols = wo_buf.shape[3]
    blocks = tok // SHIFT
    has_left, has_right = me > 0, me < n - 1
    first, last = me == 0, me == n - 1
    helps_left, helps_right = me == 1, me == n - 2
    helps = jnp.logical_or(helps_left, helps_right)
    right, left = {"wide": me + 1}, {"wide": me - 1}
    after, before = {"wide": lax.rem(me + 1, n)}, {"wide": lax.rem(me + n - 1, n)}
    opposite = {"groups": other}
    pair = {"narrow": high * 2 + 1 - low}
    others = [{"narrow": lax.rem(spot + d, narrow)} for d in range(1, narrow)]
    far = [{"narrow": lax.rem(high + d, across_n) * 2 + low} for d in range(1, across_n)]
    far_from = [{"narrow": lax.rem(high + across_n - d, across_n) * 2 + low} for d in range(1, across_n)]

    barrier = pltpu.get_barrier_semaphore()
    greeted = [after, before, opposite] + others
    for device in greeted:
        pl.semaphore_signal(barrier, inc=1, device_id=device, device_id_type=MESH)

    def w_at(shard, head, c):
        start = pl.multiple_of(shard * depth + c * rows, rows)
        return wbuf.at[head, pl.ds(start, rows)]

    def o_at(shard, part_of, c):
        return wo_buf.at[shard, part_of, pl.ds(pl.multiple_of(c * wo_rows, wo_rows), wo_rows)]

    def wo_own(c):
        return wo_ref.at[spot, y, pl.ds(pl.multiple_of(c * wo_rows, wo_rows), wo_rows)]

    def remote(src, dst, send, recv, device):
        return pltpu.make_async_remote_copy(
            src_ref=src, dst_ref=dst, send_sem=send, recv_sem=recv,
            device_id=device, device_id_type=MESH,
        )

    def q_right(shard, p, c):
        ref = w_at(shard, y * phases + p, c)
        return remote(ref, ref, qs_r.at[p, shard, c], qr.at[p, shard, c], right)

    def q_left(shard, p, c):
        ref = w_at(shard, y * phases + p, c)
        return remote(ref, ref, qs_l.at[p, shard, c], qr.at[p, shard, c], left)

    def q_across(shard, p, c, part_of):
        ref = w_at(shard, part_of * phases + p, c)
        return remote(ref, ref, qs_y.at[p, shard, c], qr_y.at[p, shard, c], opposite)

    def to_right(shard):
        return jnp.logical_and(has_right, jnp.logical_or(jnp.logical_not(helps_right), shard == me))

    def to_left(shard):
        return jnp.logical_and(has_left, jnp.logical_or(jnp.logical_not(helps_left), shard == me))

    def comes_right(s):
        return jnp.logical_and(me - 1 - s >= 0, jnp.logical_or(jnp.logical_not(last), s == 0))

    def comes_left(s):
        return jnp.logical_and(me + 1 + s <= n - 1, jnp.logical_or(jnp.logical_not(first), s == 0))

    def o_right(shard, c, src=None):
        dst = o_at(shard, y, c)
        return remote(dst if src is None else src, dst, os_r.at[shard, c], o_r.at[shard, c], right)

    def o_left(shard, c, src=None):
        dst = o_at(shard, y, c)
        return remote(dst if src is None else src, dst, os_l.at[shard, c], o_r.at[shard, c], left)

    def o_across(shard, c, part_of):
        ref = o_at(shard, part_of, c)
        return remote(ref, ref, os_y.at[shard, c], or_y.at[shard, c], opposite)

    def own_copy(head, i):
        return pltpu.make_async_copy(
            wq_ref.at[i, :, pl.ds(pl.multiple_of(head * HEAD_DIM, HEAD_DIM), HEAD_DIM)],
            wbuf.at[head, pl.ds(pl.multiple_of(me * depth, depth), depth), pl.ds(i * HEAD_DIM, HEAD_DIM)],
            own_sem.at[head, i],
        )

    order = [part_of * phases + p for p in range(phases) for part_of in (y, other)]
    for head in order:
        for i in range(3):
            own_copy(head, i).start()
    own_wo_copy = pltpu.make_async_copy(wo_ref.at[spot], wo_buf.at[me], own_wo)
    own_wo_copy.start()
    pl.semaphore_wait(barrier, len(greeted))

    far_cols = (n - 2) * depth
    my_rows = pl.ds(pl.multiple_of(spot * share, share), share)

    def lend(start, device):
        return remote(
            hidden_ref.at[my_rows, pl.ds(start, far_cols)], lent.at[my_rows],
            lend_sem.at[0], lend_sem.at[1], device,
        )

    @pl.when(first)
    def _():
        lend(2 * depth, right).start()

    @pl.when(last)
    def _():
        lend(0, left).start()

    def send_own(p):
        @pl.loop(0, chunks)
        def _(c):
            @pl.when(has_right)
            def _():
                q_right(me, p, c).start()

            @pl.when(has_left)
            def _():
                q_left(me, p, c).start()

    def send_own_wo():
        @pl.loop(0, wo_chunks)
        def _(c):
            @pl.when(has_right)
            def _():
                o_right(me, c, wo_own(c)).start()

            @pl.when(has_left)
            def _():
                o_left(me, c, wo_own(c)).start()

    def shared(d):
        return remote(
            lent.at[my_rows], lent.at[my_rows], share_s.at[d - 1], share_r.at[d - 1], others[d - 1]
        )

    def add(shard, head, c):
        start = pl.multiple_of(shard * depth + c * rows, rows)
        acc[head] += jnp.dot(
            hidden_ref[:, pl.ds(start, rows)], wbuf[head, pl.ds(start, rows)],
            preferred_element_type=jnp.float32,
        )

    def add_across(p, t):
        s, c = t // chunks, lax.rem(t, chunks)
        for there, shard in ((comes_right(s), me - 1 - s), (comes_left(s), me + 1 + s)):
            @pl.when(there)
            def _():
                q_across(shard, p, c, other).wait_recv()
                add(shard, other * phases + p, c)

    def help_copy(p, device):
        return remote(help_out.at[p], help_in.at[p], help_s.at[p], help_r.at[p], device)

    acc[...] = jnp.zeros_like(acc)
    for p in range(phases):
        if p == 0:
            for i in range(3):
                own_copy(order[0], i).wait()
            send_own(0)

            @pl.when(helps)
            def _():
                lend(0, left).wait_recv()
                for d in range(1, narrow):
                    shared(d).start()

            for head in order[1:]:
                for i in range(3):
                    own_copy(head, i).wait()

        @pl.loop(0, 2 * chunks)
        def _(i):
            add(me, i // chunks * phases + p, lax.rem(i, chunks))

        @pl.loop(0, steps)
        def _(t):
            s, c = t // chunks, lax.rem(t, chunks)

            @pl.when(comes_right(s))
            def _():
                q_right(me - 1 - s, p, c).wait_recv()

                @pl.when(to_right(me - 1 - s))
                def _():
                    q_right(me - 1 - s, p, c).start()

                q_across(me - 1 - s, p, c, y).start()

            @pl.when(comes_left(s))
            def _():
                q_left(me + 1 + s, p, c).wait_recv()

                @pl.when(to_left(me + 1 + s))
                def _():
                    q_left(me + 1 + s, p, c).start()

                q_across(me + 1 + s, p, c, y).start()

            @pl.when(t == steps - 2 * NEXT_EARLY)
            def _():
                if p + 1 < phases:
                    send_own(p + 1)

            for there, shard in ((comes_right(s), me - 1 - s), (comes_left(s), me + 1 + s)):
                @pl.when(there)
                def _():
                    add(shard, y * phases + p, c)

            @pl.when(t > 0)
            def _():
                add_across(p, t - 1)

        add_across(p, steps - 1)

        @pl.when(helps)
        def _():
            if p == 0:
                for d in range(1, narrow):
                    from_rows = pl.ds(pl.multiple_of(lax.rem(spot + narrow - d, narrow) * share, share), share)
                    remote(
                        lent.at[my_rows], lent.at[from_rows], share_s.at[d - 1], share_r.at[d - 1], others[d - 1]
                    ).wait_recv()
            start = pl.multiple_of(jnp.where(helps_left, 2 * depth, 0), depth)
            for part_of in range(2):
                help_out[p, part_of] = jnp.dot(
                    lent[...], wbuf[part_of * phases + p, pl.ds(start, far_cols)],
                    preferred_element_type=jnp.float32,
                ).astype(jnp.bfloat16)

        @pl.when(helps_left)
        def _():
            help_copy(p, left).start()

        @pl.when(helps_right)
        def _():
            help_copy(p, right).start()

    send_own_wo()
    for p in range(phases):
        @pl.when(jnp.logical_or(first, last))
        def _():
            help_copy(p, left).wait_recv()
            for part_of in range(2):
                acc[part_of * phases + p] += help_in[p, part_of].astype(jnp.float32)

    for h in range(heads):
        q_buf[h] = acc[h, :, :HEAD_DIM].astype(jnp.bfloat16)
        kv_buf[h, SHIFT:] = acc[h, :, HEAD_DIM:].astype(jnp.bfloat16)

    kv_copy = remote(
        kv_buf.at[:, pl.ds(tok, SHIFT)], kv_buf.at[:, pl.ds(0, SHIFT)],
        kv_sem.at[0], kv_sem.at[1], after,
    )
    kv_copy.start()

    causal = lax.broadcasted_iota(jnp.int32, (SHIFT, 2 * SHIFT), 1) <= (
        lax.broadcasted_iota(jnp.int32, (SHIFT, 2 * SHIFT), 0) + SHIFT
    )

    def attend(h, b):
        mine, seen = slice(b * SHIFT, (b + 1) * SHIFT), slice(b * SHIFT, (b + 2) * SHIFT)
        scores = lax.dot_general(
            q_buf[h, mine], kv_buf[h, seen, :HEAD_DIM], (((1,), (1,)), ((), ())),
            preferred_element_type=jnp.float32,
        ) * (1.0 / math.sqrt(HEAD_DIM))
        allowed = causal & (segq_ref[mine, :] == segk_ref[h, b])
        scores = jnp.where(allowed, scores, masked_out)
        exponent = jnp.exp(scores - jnp.max(scores, axis=-1, keepdims=True))
        weights = exponent / jnp.sum(exponent, axis=-1, keepdims=True)
        att[mine, h * HEAD_DIM : (h + 1) * HEAD_DIM] = jnp.dot(
            weights.astype(jnp.bfloat16), kv_buf[h, seen, HEAD_DIM:], preferred_element_type=jnp.float32
        ).astype(jnp.bfloat16)

    least = jnp.minimum(me, n - 1 - me)

    def block_of(k):
        turn = (k + 1) // 2
        near = jnp.where(lax.rem(k, 2) == 1, me - turn, me + turn)
        rest = jnp.where(me > least, me - (k - least), me + (k - least))
        return jnp.where(k <= 2 * least, near, rest)

    def pass_on(k):
        shard = block_of(k)

        @pl.loop(0, wo_chunks)
        def _(c):
            o_right(shard, c).wait_recv()

            @pl.when(jnp.logical_and(shard < me, has_right))
            def _():
                o_right(shard, c).start()

            @pl.when(jnp.logical_and(shard > me, has_left))
            def _():
                o_left(shard, c).start()

            o_across(shard, c, y).start()

    def pair_copy(shard, a):
        return remote(
            part.at[shard, a * 2 + 1 - low], pair_in.at[shard, a],
            pair_s.at[shard, a], pair_r.at[shard, a], pair,
        )

    def far_copy(shard, d):
        a = lax.rem(high + d, across_n)
        return remote(
            pair_sum.at[shard, a], far_in.at[shard, d - 1],
            far_s.at[shard, d - 1], far_r.at[shard, d - 1], far[d - 1],
        )

    def far_arrival(shard, d):
        return remote(
            pair_sum.at[shard, high], far_in.at[shard, d - 1],
            far_s.at[shard, d - 1], far_r.at[shard, d - 1], far_from[d - 1],
        )

    def multiply(k):
        shard = block_of(k)
        width = att.shape[1] // 2
        for p in range(narrow):
            a_rows = att[p * share : (p + 1) * share, :]
            total = jnp.dot(a_rows[:, :width], wo_buf[shard, 0], preferred_element_type=jnp.float32)
            total += jnp.dot(a_rows[:, width:], wo_buf[shard, 1], preferred_element_type=jnp.float32)
            part[shard, p] = total.astype(jnp.bfloat16)
        for a in range(across_n):
            pair_copy(shard, a).start()

    def sum_pair(k):
        shard = block_of(k)
        for a in range(across_n):
            pair_copy(shard, a).wait_recv()
            total = part[shard, a * 2 + low].astype(jnp.float32) + pair_in[shard, a].astype(jnp.float32)
            pair_sum[shard, a] = total.astype(jnp.bfloat16)
        for d in range(1, across_n):
            far_copy(shard, d).start()

    def finish(k):
        shard = block_of(k)
        total = part[shard, high * 2 + low].astype(jnp.float32) + pair_in[shard, high].astype(jnp.float32)
        for d in range(1, across_n):
            far_arrival(shard, d).wait_recv()
            total += far_in[shard, d - 1].astype(jnp.float32)
        out_ref[:, pl.ds(pl.multiple_of(shard * cols, cols), cols)] = total.astype(out_ref.dtype)

    for b in range(1, blocks):
        for h in range(heads):
            attend(h, b)
    pass_on(1)
    pass_on(2)
    kv_copy.wait_recv()
    for h in range(heads):
        attend(h, 0)
    own_wo_copy.wait()
    multiply(0)

    @pl.loop(1, n)
    def _(k):
        @pl.when(k > 2)
        def _():
            pass_on(k)

        sum_pair(k - 1)

        @pl.when(k > 1)
        def _():
            finish(k - 2)

        shard = block_of(k)

        @pl.loop(0, wo_chunks)
        def _(c):
            o_across(shard, c, other).wait_recv()

        multiply(k)

    sum_pair(n - 1)
    finish(n - 2)
    finish(n - 1)

    kv_copy.wait_send()

    @pl.loop(0, n)
    def _(shard):
        for a in range(across_n):
            pair_copy(shard, a).wait_send()
        for d in range(1, across_n):
            far_copy(shard, d).wait_send()
        @pl.loop(0, chunks)
        def _(c):
            for p in range(phases):
                @pl.when(jnp.logical_and(shard <= me, to_right(shard)))
                def _():
                    q_right(shard, p, c).wait_send()

                @pl.when(jnp.logical_and(shard >= me, to_left(shard)))
                def _():
                    q_left(shard, p, c).wait_send()

                came = jnp.where(shard < me, comes_right(me - 1 - shard), comes_left(shard - me - 1))

                @pl.when(jnp.logical_and(shard != me, came))
                def _():
                    q_across(shard, p, c, y).wait_send()

        @pl.loop(0, wo_chunks)
        def _(c):
            @pl.when(jnp.logical_and(shard <= me, has_right))
            def _():
                o_right(shard, c).wait_send()

            @pl.when(jnp.logical_and(shard >= me, has_left))
            def _():
                o_left(shard, c).wait_send()

            @pl.when(shard != me)
            def _():
                o_across(shard, c, y).wait_send()

    @pl.when(jnp.logical_or(first, last))
    def _():
        lend(0, left).wait_send()

    @pl.when(helps)
    def _():
        for d in range(1, narrow):
            shared(d).wait_send()
        for p in range(phases):
            help_copy(p, left).wait_send()


def layer(hidden, wq, wo, seg_q, seg_k):
    n, narrow = lax.axis_size("wide"), lax.axis_size("narrow")
    tok, width = hidden.shape
    depth = wq.shape[1]
    heads = wq.shape[2] // HEAD_DIM
    phases = heads // 2
    chunks = max(1, depth // ROWS)
    wo_chunks = WO_CHUNKS
    cols = wo.shape[3]
    share = tok // narrow
    vmem = pl.BlockSpec(memory_space=pltpu.VMEM)
    hbm = pl.BlockSpec(memory_space=pl.ANY)
    dma = pltpu.SemaphoreType.DMA
    bf16 = jnp.bfloat16
    return pl.pallas_call(
        functools.partial(layer_kernel, n, narrow, chunks, wo_chunks),
        out_shape=jax.ShapeDtypeStruct((share, n * cols), bf16),
        in_specs=[vmem, hbm, hbm, vmem, vmem],
        out_specs=vmem,
        scratch_shapes=[
            pltpu.VMEM((heads, width, 3 * HEAD_DIM), bf16),
            pltpu.VMEM((heads, tok, 3 * HEAD_DIM), jnp.float32),
            pltpu.VMEM((n,) + wo.shape[1:], bf16),
            pltpu.VMEM((heads, tok, HEAD_DIM), bf16),
            pltpu.VMEM((heads, tok + SHIFT, 2 * HEAD_DIM), bf16),
            pltpu.VMEM((tok, heads * HEAD_DIM), bf16),
            pltpu.VMEM((n, narrow, share, cols), bf16),
            pltpu.VMEM((n, narrow // 2, share, cols), bf16),
            pltpu.VMEM((n, narrow // 2, share, cols), bf16),
            pltpu.VMEM((n, max(1, narrow // 2 - 1), share, cols), bf16),
            pltpu.VMEM((tok, (n - 2) * depth), bf16),
            pltpu.VMEM((phases, 2, tok, 3 * HEAD_DIM), bf16),
            pltpu.VMEM((phases, 2, tok, 3 * HEAD_DIM), bf16),
            dma((heads, 3)),
            dma(()),
        ]
        + [dma((phases, n, chunks))] * 5
        + [dma((n, wo_chunks))] * 5
        + [dma((2,))]
        + [dma((n, narrow // 2))] * 2
        + [dma((n, max(1, narrow // 2 - 1)))] * 2
        + [dma((2,))]
        + [dma((narrow - 1,))] * 2
        + [dma((phases,))] * 2,
        compiler_params=pltpu.CompilerParams(
            collective_id=0, has_side_effects=True, vmem_limit_bytes=58 * 1024 * 1024
        ),
    )(hidden, wq, wo, seg_q, seg_k)


def per_device(hidden, w_qkv, w_out, seg_ids, shift_heads):
    tok_rows = hidden.shape[0]
    local_f = w_qkv.shape[2]
    heads_here = local_f // HEAD_DIM
    blocks = tok_rows // SHIFT
    narrow = lax.axis_size("narrow")
    first_tok = lax.axis_index("wide") * tok_rows
    shifted = lax.dynamic_slice_in_dim(shift_heads, lax.axis_index("narrow") * heads_here, heads_here) > 0

    doubled = jnp.concatenate([seg_ids[-SHIFT:], seg_ids], 0)
    seg_here = lax.dynamic_slice_in_dim(doubled, first_tok, tok_rows + SHIFT)
    seg_q = seg_here[SHIFT:, None]
    windows = jnp.stack([seg_here[b * SHIFT : (b + 2) * SHIFT] for b in range(blocks)])
    odd = (jnp.arange(blocks) % 2 == 1)[None, :, None]
    reaches = (shifted[:, None, None] != odd) | (jnp.arange(2 * SHIFT) >= SHIFT)[None, None, :]
    seg_k = jnp.where(reaches, windows[None], -1)[:, :, None, :]

    wq = w_qkv.transpose(1, 0, 2)
    wo = w_out.reshape(narrow, 2, local_f // 2, -1)
    return layer(hidden, wq, wo, seg_q, seg_k)


def solution(mesh):
    placed = (
        P(("groups", "wide"), None),
        P("wide", None, "narrow"),
        P(None, "wide"),
        P("groups"),
        P(),
    )
    return jax.shard_map(
        per_device,
        mesh=mesh,
        in_specs=placed,
        out_specs=P(("groups", "wide", "narrow"), None),
        check_vma=False,
    )
```

```python
import functools
import math

import jax
import jax.numpy as jnp
from jax import lax
from jax.experimental import pallas as pl
from jax.experimental.pallas import tpu as pltpu
from jax.sharding import PartitionSpec as P

HEAD_DIM = 128
GROUP = 512
SHIFT = 256

masked_out = -1e30
MESH = pl.DeviceIdType.MESH
ROWS = 128
WO_CHUNKS = 4


def layer_kernel(
    n, narrow, chunks, wo_chunks,
    hidden_ref, wq_ref, wo_ref, segq_ref, segk_ref, out_ref,
    wbuf, acc, wo_buf, q_buf, kv_buf, att, part, pair_in, pair_sum, far_in,
    own_sem,
    qs_r, qs_l, qr, qs_y, qr_y,
    os_r, os_l, o_r, os_y, or_y,
    kv_sem, pair_s, pair_r, far_s, far_r,
):
    me = lax.axis_index("wide")
    y = lax.axis_index("groups")
    spot = lax.axis_index("narrow")
    other = 1 - y
    across_n = narrow // 2
    high, low = spot // 2, lax.rem(spot, 2)
    depth = wq_ref.shape[1]
    half = wbuf.shape[3]
    tok = hidden_ref.shape[0]
    rows = depth // chunks
    steps = (n - 1) * chunks
    wo_rows = wo_buf.shape[2] // wo_chunks
    cols = wo_buf.shape[3]
    blocks = tok // SHIFT
    per_half = half // HEAD_DIM
    has_left, has_right = me > 0, me < n - 1
    right, left = {"wide": me + 1}, {"wide": me - 1}
    after, before = {"wide": lax.rem(me + 1, n)}, {"wide": lax.rem(me + n - 1, n)}
    opposite = {"groups": other}
    pair = {"narrow": high * 2 + 1 - low}
    far = [{"narrow": lax.rem(high + d, across_n) * 2 + low} for d in range(1, across_n)]
    far_from = [{"narrow": lax.rem(high + across_n - d, across_n) * 2 + low} for d in range(1, across_n)]

    barrier = pltpu.get_barrier_semaphore()
    greeted = [after, before, opposite, pair] + far
    for device in greeted:
        pl.semaphore_signal(barrier, inc=1, device_id=device, device_id_type=MESH)

    def w_at(shard, part_of, c):
        start = pl.multiple_of(shard * depth + c * rows, rows)
        return wbuf.at[part_of, :, pl.ds(start, rows)]

    def wq_own(c):
        return wq_ref.at[
            :, pl.ds(pl.multiple_of(c * rows, rows), rows), pl.ds(pl.multiple_of(y * half, half), half)
        ]

    def o_at(shard, part_of, c):
        return wo_buf.at[shard, part_of, pl.ds(pl.multiple_of(c * wo_rows, wo_rows), wo_rows)]

    def wo_own(c):
        return wo_ref.at[spot, y, pl.ds(pl.multiple_of(c * wo_rows, wo_rows), wo_rows)]

    def remote(src, dst, send, recv, device):
        return pltpu.make_async_remote_copy(
            src_ref=src, dst_ref=dst, send_sem=send, recv_sem=recv,
            device_id=device, device_id_type=MESH,
        )

    def q_right(shard, c, src=None):
        dst = w_at(shard, y, c)
        return remote(dst if src is None else src, dst, qs_r.at[shard, c], qr.at[shard, c], right)

    def q_left(shard, c, src=None):
        dst = w_at(shard, y, c)
        return remote(dst if src is None else src, dst, qs_l.at[shard, c], qr.at[shard, c], left)

    def q_across(shard, c, part_of):
        ref = w_at(shard, part_of, c)
        return remote(ref, ref, qs_y.at[shard, c], qr_y.at[shard, c], opposite)

    def o_right(shard, c, src=None):
        dst = o_at(shard, y, c)
        return remote(dst if src is None else src, dst, os_r.at[shard, c], o_r.at[shard, c], right)

    def o_left(shard, c, src=None):
        dst = o_at(shard, y, c)
        return remote(dst if src is None else src, dst, os_l.at[shard, c], o_r.at[shard, c], left)

    def o_across(shard, c, part_of):
        ref = o_at(shard, part_of, c)
        return remote(ref, ref, os_y.at[shard, c], or_y.at[shard, c], opposite)

    own = [
        pltpu.make_async_copy(
            wq_ref.at[:, :, pl.ds(h * half, half)],
            wbuf.at[h, :, pl.ds(pl.multiple_of(me * depth, depth), depth)],
            own_sem.at[h],
        )
        for h in range(2)
    ]
    own.append(pltpu.make_async_copy(wo_ref.at[spot], wo_buf.at[me], own_sem.at[2]))
    for copy in own:
        copy.start()
    pl.semaphore_wait(barrier, len(greeted))

    @pl.loop(0, chunks)
    def _(c):
        @pl.when(has_right)
        def _():
            q_right(me, c, wq_own(c)).start()

        @pl.when(has_left)
        def _():
            q_left(me, c, wq_own(c)).start()

    acc[...] = jnp.zeros_like(acc)
    own[0].wait()
    own[1].wait()

    def add(shard, part_of, c):
        start = pl.multiple_of(shard * depth + c * rows, rows)
        piece = hidden_ref[:, pl.ds(start, rows)]
        for i in range(3):
            acc[part_of, i] += jnp.dot(
                piece, wbuf[part_of, i, pl.ds(start, rows)], preferred_element_type=jnp.float32
            )

    @pl.loop(0, 2 * chunks)
    def _(i):
        add(me, i // chunks, lax.rem(i, chunks))

    def add_across(t):
        s, c = t // chunks, lax.rem(t, chunks)
        for there, shard in ((me - 1 - s >= 0, me - 1 - s), (me + 1 + s <= n - 1, me + 1 + s)):
            @pl.when(there)
            def _():
                q_across(shard, c, other).wait_recv()
                add(shard, other, c)

    def send_own_wo():
        @pl.loop(0, wo_chunks)
        def _(c):
            @pl.when(has_right)
            def _():
                o_right(me, c, wo_own(c)).start()

            @pl.when(has_left)
            def _():
                o_left(me, c, wo_own(c)).start()

    @pl.loop(0, steps)
    def _(t):
        s, c = t // chunks, lax.rem(t, chunks)

        @pl.when(t == steps - chunks)
        def _():
            send_own_wo()

        @pl.when(me - 1 - s >= 0)
        def _():
            q_right(me - 1 - s, c).wait_recv()

            @pl.when(has_right)
            def _():
                q_right(me - 1 - s, c).start()

            q_across(me - 1 - s, c, y).start()

        @pl.when(me + 1 + s <= n - 1)
        def _():
            q_left(me + 1 + s, c).wait_recv()

            @pl.when(has_left)
            def _():
                q_left(me + 1 + s, c).start()

            q_across(me + 1 + s, c, y).start()

        for there, shard in ((me - 1 - s >= 0, me - 1 - s), (me + 1 + s <= n - 1, me + 1 + s)):
            @pl.when(there)
            def _():
                add(shard, y, c)

        @pl.when(t > 0)
        def _():
            add_across(t - 1)

    add_across(steps - 1)
    for h in range(2):
        q_buf[h] = acc[h, 0].astype(jnp.bfloat16)
        for i in range(2):
            kv_buf[h, i, SHIFT:] = acc[h, 1 + i].astype(jnp.bfloat16)

    kv_copy = remote(
        kv_buf.at[:, :, pl.ds(tok, SHIFT)], kv_buf.at[:, :, pl.ds(0, SHIFT)],
        kv_sem.at[0], kv_sem.at[1], after,
    )
    kv_copy.start()

    causal = lax.broadcasted_iota(jnp.int32, (SHIFT, 2 * SHIFT), 1) <= (
        lax.broadcasted_iota(jnp.int32, (SHIFT, 2 * SHIFT), 0) + SHIFT
    )

    def attend(h, b):
        lanes = slice((h % per_half) * HEAD_DIM, (h % per_half + 1) * HEAD_DIM)
        mine, seen = slice(b * SHIFT, (b + 1) * SHIFT), slice(b * SHIFT, (b + 2) * SHIFT)
        keys, values = kv_buf.at[h // per_half, 0], kv_buf.at[h // per_half, 1]
        scores = lax.dot_general(
            q_buf[h // per_half, mine, lanes], keys[seen, lanes], (((1,), (1,)), ((), ())),
            preferred_element_type=jnp.float32,
        ) * (1.0 / math.sqrt(HEAD_DIM))
        allowed = causal & (segq_ref[mine, :] == segk_ref[h, b])
        scores = jnp.where(allowed, scores, masked_out)
        exponent = jnp.exp(scores - jnp.max(scores, axis=-1, keepdims=True))
        weights = exponent / jnp.sum(exponent, axis=-1, keepdims=True)
        att[mine, h * HEAD_DIM : (h + 1) * HEAD_DIM] = jnp.dot(
            weights.astype(jnp.bfloat16), values[seen, lanes], preferred_element_type=jnp.float32
        ).astype(jnp.bfloat16)

    least = jnp.minimum(me, n - 1 - me)

    def block_of(k):
        turn = (k + 1) // 2
        near = jnp.where(lax.rem(k, 2) == 1, me - turn, me + turn)
        rest = jnp.where(me > least, me - (k - least), me + (k - least))
        return jnp.where(k <= 2 * least, near, rest)

    def pass_on(k):
        shard = block_of(k)

        @pl.loop(0, wo_chunks)
        def _(c):
            o_right(shard, c).wait_recv()

            @pl.when(jnp.logical_and(shard < me, has_right))
            def _():
                o_right(shard, c).start()

            @pl.when(jnp.logical_and(shard > me, has_left))
            def _():
                o_left(shard, c).start()

            o_across(shard, c, y).start()

    def pair_copy(shard, a):
        return remote(
            part.at[shard, a * 2 + 1 - low], pair_in.at[shard, a],
            pair_s.at[shard, a], pair_r.at[shard, a], pair,
        )

    def far_copy(shard, d):
        a = lax.rem(high + d, across_n)
        return remote(
            pair_sum.at[shard, a], far_in.at[shard, d - 1],
            far_s.at[shard, d - 1], far_r.at[shard, d - 1], far[d - 1],
        )

    def far_arrival(shard, d):
        return remote(
            pair_sum.at[shard, high], far_in.at[shard, d - 1],
            far_s.at[shard, d - 1], far_r.at[shard, d - 1], far_from[d - 1],
        )

    def multiply(k):
        shard = block_of(k)
        width = att.shape[1] // 2
        share = tok // narrow
        for p in range(narrow):
            a_rows = att[p * share : (p + 1) * share, :]
            total = jnp.dot(a_rows[:, :width], wo_buf[shard, 0], preferred_element_type=jnp.float32)
            total += jnp.dot(a_rows[:, width:], wo_buf[shard, 1], preferred_element_type=jnp.float32)
            part[shard, p] = total.astype(jnp.bfloat16)
        for a in range(across_n):
            pair_copy(shard, a).start()

    def sum_pair(k):
        shard = block_of(k)
        for a in range(across_n):
            pair_copy(shard, a).wait_recv()
            total = part[shard, a * 2 + low].astype(jnp.float32) + pair_in[shard, a].astype(jnp.float32)
            pair_sum[shard, a] = total.astype(jnp.bfloat16)
        for d in range(1, across_n):
            far_copy(shard, d).start()

    def finish(k):
        shard = block_of(k)
        total = part[shard, high * 2 + low].astype(jnp.float32) + pair_in[shard, high].astype(jnp.float32)
        for d in range(1, across_n):
            far_arrival(shard, d).wait_recv()
            total += far_in[shard, d - 1].astype(jnp.float32)
        out_ref[:, pl.ds(pl.multiple_of(shard * cols, cols), cols)] = total.astype(out_ref.dtype)

    heads = 2 * per_half
    for b in range(1, blocks):
        for h in range(heads):
            attend(h, b)
    pass_on(1)
    pass_on(2)
    kv_copy.wait_recv()
    for h in range(heads):
        attend(h, 0)
    own[2].wait()
    multiply(0)

    @pl.loop(1, n)
    def _(k):
        @pl.when(k > 2)
        def _():
            pass_on(k)

        sum_pair(k - 1)

        @pl.when(k > 1)
        def _():
            finish(k - 2)

        shard = block_of(k)

        @pl.loop(0, wo_chunks)
        def _(c):
            o_across(shard, c, other).wait_recv()

        multiply(k)

    sum_pair(n - 1)
    finish(n - 2)
    finish(n - 1)

    kv_copy.wait_send()

    @pl.loop(0, n)
    def _(shard):
        for a in range(across_n):
            pair_copy(shard, a).wait_send()
        for d in range(1, across_n):
            far_copy(shard, d).wait_send()
        goes_right = jnp.logical_and(shard <= me, has_right)
        goes_left = jnp.logical_and(shard >= me, has_left)
        for count, to_right, to_left, to_other in (
            (chunks, q_right, q_left, q_across), (wo_chunks, o_right, o_left, o_across)
        ):
            @pl.loop(0, count)
            def _(c):
                @pl.when(goes_right)
                def _():
                    to_right(shard, c).wait_send()

                @pl.when(goes_left)
                def _():
                    to_left(shard, c).wait_send()

                @pl.when(shard != me)
                def _():
                    to_other(shard, c, y).wait_send()


def layer(hidden, wq, wo, seg_q, seg_k):
    n, narrow = lax.axis_size("wide"), lax.axis_size("narrow")
    tok, width = hidden.shape
    half = wq.shape[2] // 2
    chunks = max(1, wq.shape[1] // ROWS)
    wo_chunks = WO_CHUNKS
    cols = wo.shape[3]
    share = tok // narrow
    vmem = pl.BlockSpec(memory_space=pltpu.VMEM)
    hbm = pl.BlockSpec(memory_space=pl.ANY)
    dma = pltpu.SemaphoreType.DMA
    bf16 = jnp.bfloat16
    return pl.pallas_call(
        functools.partial(layer_kernel, n, narrow, chunks, wo_chunks),
        out_shape=jax.ShapeDtypeStruct((share, n * cols), bf16),
        in_specs=[vmem, hbm, hbm, vmem, vmem],
        out_specs=vmem,
        scratch_shapes=[
            pltpu.VMEM((2, 3, width, half), bf16),
            pltpu.VMEM((2, 3, tok, half), jnp.float32),
            pltpu.VMEM((n,) + wo.shape[1:], bf16),
            pltpu.VMEM((2, tok, half), bf16),
            pltpu.VMEM((2, 2, tok + SHIFT, half), bf16),
            pltpu.VMEM((tok, 2 * half), bf16),
            pltpu.VMEM((n, narrow, share, cols), bf16),
            pltpu.VMEM((n, narrow // 2, share, cols), bf16),
            pltpu.VMEM((n, narrow // 2, share, cols), bf16),
            pltpu.VMEM((n, max(1, narrow // 2 - 1), share, cols), bf16),
            dma((3,)),
        ]
        + [dma((n, chunks))] * 5
        + [dma((n, wo_chunks))] * 5
        + [dma((2,))]
        + [dma((n, narrow // 2))] * 2
        + [dma((n, max(1, narrow // 2 - 1)))] * 2,
        compiler_params=pltpu.CompilerParams(
            collective_id=0, has_side_effects=True, vmem_limit_bytes=58 * 1024 * 1024
        ),
    )(hidden, wq, wo, seg_q, seg_k)


def per_device(hidden, w_qkv, w_out, seg_ids, shift_heads):
    tok_rows = hidden.shape[0]
    local_f = w_qkv.shape[2]
    heads_here = local_f // HEAD_DIM
    blocks = tok_rows // SHIFT
    narrow = lax.axis_size("narrow")
    first_tok = lax.axis_index("wide") * tok_rows
    shifted = lax.dynamic_slice_in_dim(shift_heads, lax.axis_index("narrow") * heads_here, heads_here) > 0

    doubled = jnp.concatenate([seg_ids[-SHIFT:], seg_ids], 0)
    seg_here = lax.dynamic_slice_in_dim(doubled, first_tok, tok_rows + SHIFT)
    seg_q = seg_here[SHIFT:, None]
    windows = jnp.stack([seg_here[b * SHIFT : (b + 2) * SHIFT] for b in range(blocks)])
    odd = (jnp.arange(blocks) % 2 == 1)[None, :, None]
    reaches = (shifted[:, None, None] != odd) | (jnp.arange(2 * SHIFT) >= SHIFT)[None, None, :]
    seg_k = jnp.where(reaches, windows[None], -1)[:, :, None, :]

    wq = w_qkv.transpose(1, 0, 2)
    wo = w_out.reshape(narrow, 2, local_f // 2, -1)
    return layer(hidden, wq, wo, seg_q, seg_k)


def solution(mesh):
    placed = (
        P(("groups", "wide"), None),
        P("wide", None, "narrow"),
        P(None, "wide"),
        P("groups"),
        P(),
    )
    return jax.shard_map(
        per_device,
        mesh=mesh,
        in_specs=placed,
        out_specs=P(("groups", "wide", "narrow"), None),
        check_vma=False,
    )
```
